32 devices in a mesh: scan: 4 (over z), tx: 4 (over y, x), ty: 2 (over core).
Axes of the slice: x: 2, y: 2, z: 4, core: 2. Of those that a mesh axis runs over, the one named last changes fastest.
Arguments:
- object_slices: float32 [2, 2, 1024, 512], P(None, None, 'tx', 'ty'), may hold values from -0.9 to 0.9
- probe_modes: float32 [2, 8, 256, 256], replicated, may hold values from -1.2 to 1.2
- corners: int32 [4, 2, 4, 2], P('tx', 'ty', 'scan'), may hold values from 0 to 127, as said below
- measured: float32 [4, 2, 4, 256, 256], P('tx', 'ty', 'scan'), may hold values from 0.2 to 2.5
Outputs:
- updated_object: float32 [2, 2, 1024, 512], P(None, None, 'tx', 'ty')
The draws below stay inside these ranges and needn't reach their ends.
Inputs may be any that keep to these rules, and one draw needn't show every extreme that they name: corners place every window inside its own tile and the 128 pixels below and to the right of it.
All inputs are finite; a program needn't handle non-finite values.
Results may differ from the reference program's by a relative error of at most 0.0001.
Values sent between devices are 32-bit elements; how exact they have to be, the bound alone decides.
A program may use at most 64 MiB of HBM per device.

```python
import jax
import jax.numpy as jnp
from jax import lax

P_SIZE = 256
MODES = 8
SLICES = 2
ITERS = 1
TILE = 256
SCANS = 4
NY = 1024
NX = 512
N_TX = 4
N_TY = 2


def draw_corners(key, part):
    corner_span = TILE - P_SIZE + P_SIZE // 2
    drawn = jax.random.randint(key, (N_TX, N_TY, SCANS, 2), 0, corner_span, dtype=jnp.int32)
    drawn = drawn.at[0, 0, 0, :].set(0)
    return drawn.at[N_TX - 1, N_TY - 1, SCANS - 1, :].set(corner_span - 1)


def steps_of(own_key, extent, cuts, smallest, high):
    gain = 1.0
    for dim, parts in cuts:
        heights = jax.random.uniform(jax.random.fold_in(jax.random.fold_in(own_key, 6), dim), (parts,), jnp.float32, smallest / len(cuts), high / len(cuts))
        gain = gain * jnp.repeat(jnp.exp(heights), extent[dim] // parts).reshape((-1,) + (1,) * (len(extent) - 1 - dim))
    return gain


def scatter_about(rng, dims, width, limit, cuts=(), kind=jnp.bfloat16):
    gain = steps_of(rng, dims, cuts, -0.22, 0.18) if cuts else 1.0
    array = jax.random.normal(rng, dims, jnp.float32) * width * gain
    return jnp.minimum(jnp.maximum(array, -limit), limit).astype(kind)


def setup_inputs(seed: int = 0) -> dict:
    streams_of = jax.random.split(jax.random.key(seed), 5)
    return {
        "object_slices": scatter_about(streams_of[0], (SLICES, 2, NY, NX), 0.15, 0.9, ((2, 4), (3, 2)), jnp.float32),
        "probe_modes": scatter_about(streams_of[1], (2, MODES, P_SIZE, P_SIZE), 0.2, 1.2, (), jnp.float32),
        "corners": draw_corners(jax.random.fold_in(streams_of[4], 71), 0),
        "measured": jnp.clip(0.2 + 2.3 * jax.random.uniform(streams_of[3], (N_TX, N_TY, SCANS, P_SIZE, P_SIZE), jnp.float32) ** steps_of(streams_of[3], (N_TX, N_TY, SCANS, P_SIZE, P_SIZE), ((0, 4), (1, 2), (2, 4)), -0.2, 0.2), 0.2, 2.5),
    }


fresnel_coef = 0.1
step_size = 4.0


def laplacian(field):
    padded = jnp.pad(field, ((0, 0), (1, 1), (1, 1)))
    return padded[:, :-2, 1:-1] + padded[:, 2:, 1:-1] + padded[:, 1:-1, :-2] + padded[:, 1:-1, 2:] - 4.0 * field


def propagate(field, sign_value):
    lap_once = laplacian(field)
    lap_twice = laplacian(lap_once)
    return field + (sign_value * fresnel_coef * 1j) * lap_once - (0.5 * fresnel_coef ** 2) * lap_twice


def position_terms(padded_obj, probe_complex, row_start, col_start, measured_one):
    zero_index = jnp.zeros((), jnp.int32)
    window = lax.dynamic_slice(padded_obj, (zero_index, row_start, col_start), (SLICES, P_SIZE, P_SIZE))
    transmit = 1.0 + window
    stored = []
    field_now = probe_complex
    exit_wave = field_now
    for layer_index in range(SLICES):
        stored.append(field_now)
        exit_wave = field_now * transmit[layer_index]
        if layer_index + 1 < SLICES:
            field_now = propagate(exit_wave, 1.0)
    far_field = jnp.fft.fft2(exit_wave, norm="ortho")
    misfit = jnp.sum(jnp.real(far_field) ** 2 + jnp.imag(far_field) ** 2, axis=0) - measured_one
    backward = jnp.fft.ifft2(2.0 * misfit * far_field, norm="ortho")
    gradients = [None] * SLICES
    for layer_index in reversed(range(SLICES)):
        field_now = stored[layer_index]
        grad_term = jnp.sum(jnp.conj(field_now) * backward, axis=0)
        lighting = jnp.sum(jnp.real(field_now) ** 2 + jnp.imag(field_now) ** 2, axis=0)
        gradients[layer_index] = jnp.stack([jnp.real(grad_term), jnp.imag(grad_term), lighting])
        if layer_index > 0:
            backward = propagate(jnp.conj(transmit[layer_index]) * backward, -1.0)
    return jnp.stack(gradients)


def reference(object_slices, probe_modes, corners, measured):
    rim_width = P_SIZE // 2
    probe_complex = lax.complex(probe_modes[0], probe_modes[1])
    row_base = (jnp.arange(N_TX, dtype=jnp.int32) * TILE)[:, None, None]
    col_base = (jnp.arange(N_TY, dtype=jnp.int32) * TILE)[None, :, None]
    row_starts = (row_base + corners[..., 0]).reshape(-1).astype(jnp.int32)
    col_starts = (col_base + corners[..., 1]).reshape(-1).astype(jnp.int32)
    measured_flat = measured.reshape(-1, P_SIZE, P_SIZE)
    current = object_slices
    for iteration in range(ITERS):
        padded_obj = jnp.pad(lax.complex(current[:, 0], current[:, 1]), ((0, 0), (0, rim_width), (0, rim_width)))

        def visit(accumulated, item):
            row_start, col_start, measured_one = item
            grad_terms = position_terms(padded_obj, probe_complex, row_start, col_start, measured_one)
            zero_index = jnp.zeros((), jnp.int32)
            starts = (zero_index, zero_index, row_start, col_start)
            updated = lax.dynamic_slice(accumulated, starts, grad_terms.shape) + grad_terms
            return lax.dynamic_update_slice(accumulated, updated, starts), None

        initial = jnp.zeros((SLICES, 3, NY + rim_width, NX + rim_width), jnp.float32)
        accumulated = lax.scan(visit, initial, (row_starts, col_starts, measured_flat))[0]
        summed = accumulated[:, :, :NY, :NX]
        current = current - step_size * summed[:, :2] / (summed[:, 2:3] + 1.0)
    return current
```

```python
import functools
import math

import jax
import jax.numpy as jnp
import numpy as np
from jax import lax
from jax.experimental import pallas as pl
from jax.experimental.pallas import tpu as pltpu
from jax.sharding import PartitionSpec as P

fresnel_coef = 0.1
step_size = 4.0
damping = 0.5 * fresnel_coef**2


def dft_tables(pixels):
    half = pixels // 2
    tables = []
    for parity in range(2):
        freq = 2 * np.arange(half) + parity
        angle = 2.0 * np.pi * ((freq[:, None] * np.arange(half)[None, :]) % pixels) / pixels
        c, s = np.cos(angle) / math.sqrt(pixels), np.sin(angle) / math.sqrt(pixels)
        tables.append(np.block([[c, s], [-s, c]]))
    tables += [t.T for t in tables]
    out = []
    for t in tables:
        t32 = t.astype(np.float32)
        high = t32.astype(jnp.bfloat16)
        low = (t - high.astype(np.float64)).astype(np.float32).astype(jnp.bfloat16)
        out += [high, low]
    return np.stack(out)


def split2(x):
    high = x.astype(jnp.bfloat16)
    return high, (x - high.astype(jnp.float32)).astype(jnp.bfloat16)


def right_dot(x, high, low):
    xh, xl = split2(x)
    lhs = jnp.concatenate([xh, xl, xh], axis=1)
    rhs = jnp.concatenate([high, high, low], axis=0)
    return jnp.dot(lhs, rhs, preferred_element_type=jnp.float32)


def left_dot(high, low, x):
    xh, xl = split2(x)
    lhs = jnp.concatenate([high, high, low], axis=1)
    rhs = jnp.concatenate([xh, xl, xh], axis=0)
    return jnp.dot(lhs, rhs, preferred_element_type=jnp.float32)


def propagate(re, im, sign, edges):
    first_row, last_row, first_col, last_col = edges
    n = re.shape[0]

    def lap(v):
        up = jnp.where(first_row, 0.0, pltpu.roll(v, 1, 0))
        down = jnp.where(last_row, 0.0, pltpu.roll(v, n - 1, 0))
        left = jnp.where(first_col, 0.0, pltpu.roll(v, 1, 1))
        right = jnp.where(last_col, 0.0, pltpu.roll(v, n - 1, 1))
        return (up + down) + (left + right) - 4.0 * v

    l_re, l_im = lap(re), lap(im)
    ll_re, ll_im = lap(l_re), lap(l_im)
    coef = sign * fresnel_coef
    return re - coef * l_im - damping * ll_re, im + coef * l_re - damping * ll_im


def position_kernel(
    corner, ext, probe, measured, tables, acc, trans, wave1, far, misfit, sums, padded
):
    modes, n = probe.shape[1], probe.shape[2]
    h = n // 2
    r, c = corner[0], corner[1]
    wide = ext.shape[2]
    up, left = jnp.where(r == 0, 0, wide - r), jnp.where(c == 0, 0, wide - c)
    for p in range(4):
        rows = pltpu.roll(ext[p], up, 0)[:n]
        window = pltpu.roll(rows, left, 1)[:, :n]
        trans[p] = window + 1.0 if p % 2 == 0 else window
    row = lax.broadcasted_iota(jnp.int32, (n, n), 0)
    col = lax.broadcasted_iota(jnp.int32, (n, n), 1)
    edges = (row == 0, row == n - 1, col == 0, col == n - 1)
    one_hot = jnp.where(col == jnp.where(row < h, 2 * row, 2 * (row - h) + 1), 1.0, 0.0)
    one_hot_t = jnp.where(row == jnp.where(col < h, 2 * col, 2 * (col - h) + 1), 1.0, 0.0)

    def three(x):
        hi, rest = split2(x)
        mid = rest
        lo = (x - hi.astype(jnp.float32) - mid.astype(jnp.float32)).astype(jnp.bfloat16)
        return hi, mid, lo

    ph, pt = one_hot.astype(jnp.bfloat16), one_hot_t.astype(jnp.bfloat16)
    half_done = sum(
        jnp.dot(ph, part, preferred_element_type=jnp.float32) for part in three(measured[...])
    )
    misfit[...] = -sum(
        jnp.dot(part, pt, preferred_element_type=jnp.float32) for part in three(half_done)
    )
    sums[...] = jnp.zeros_like(sums)

    def forward(m, _):
        re0, im0 = probe[0, m], probe[1, m]
        sums[2] += re0 * re0 + im0 * im0
        tr, ti = trans[0], trans[1]
        re1, im1 = propagate(re0 * tr - im0 * ti, re0 * ti + im0 * tr, 1.0, edges)
        wave1[0, m] = re1
        wave1[1, m] = im1
        sums[5] += re1 * re1 + im1 * im1
        tr, ti = trans[2], trans[3]
        er, ei = re1 * tr - im1 * ti, re1 * ti + im1 * tr
        even = right_dot(
            jnp.concatenate([er[:, :h] + er[:, h:], ei[:, :h] + ei[:, h:]], axis=1),
            tables[4], tables[5],
        )
        odd = right_dot(
            jnp.concatenate([er[:, :h] - er[:, h:], ei[:, :h] - ei[:, h:]], axis=1),
            tables[6], tables[7],
        )
        fr = jnp.concatenate([even[:, :h], odd[:, :h]], axis=1)
        fi = jnp.concatenate([even[:, h:], odd[:, h:]], axis=1)
        f_even = left_dot(
            tables[0], tables[1],
            jnp.concatenate([fr[:h] + fr[h:], fi[:h] + fi[h:]], axis=0),
        )
        f_odd = left_dot(
            tables[2], tables[3],
            jnp.concatenate([fr[:h] - fr[h:], fi[:h] - fi[h:]], axis=0),
        )
        far[0, m] = f_even
        far[1, m] = f_odd
        misfit[:h] += f_even[:h] * f_even[:h] + f_even[h:] * f_even[h:]
        misfit[h:] += f_odd[:h] * f_odd[:h] + f_odd[h:] * f_odd[h:]
        return 0

    lax.fori_loop(0, modes, forward, 0)

    def backward(m, _):
        m_even, m_odd = 2.0 * misfit[:h], 2.0 * misfit[h:]
        b_even = left_dot(
            tables[4], tables[5], far[0, m] * jnp.concatenate([m_even, m_even], axis=0)
        )
        b_odd = left_dot(
            tables[6], tables[7], far[1, m] * jnp.concatenate([m_odd, m_odd], axis=0)
        )
        top, low = b_even + b_odd, b_even - b_odd
        br = jnp.concatenate([top[:h], low[:h]], axis=0)
        bi = jnp.concatenate([top[h:], low[h:]], axis=0)
        c_even = right_dot(
            jnp.concatenate([br[:, :h], bi[:, :h]], axis=1), tables[0], tables[1]
        )
        c_odd = right_dot(
            jnp.concatenate([br[:, h:], bi[:, h:]], axis=1), tables[2], tables[3]
        )
        lo, hi = c_even + c_odd, c_even - c_odd
        br = jnp.concatenate([lo[:, :h], hi[:, :h]], axis=1)
        bi = jnp.concatenate([lo[:, h:], hi[:, h:]], axis=1)
        wr, wi = wave1[0, m], wave1[1, m]
        sums[3] += wr * br + wi * bi
        sums[4] += wr * bi - wi * br
        tr, ti = trans[2], trans[3]
        br, bi = propagate(tr * br + ti * bi, tr * bi - ti * br, -1.0, edges)
        wr, wi = probe[0, m], probe[1, m]
        sums[0] += wr * br + wi * bi
        sums[1] += wr * bi - wi * br
        return 0

    lax.fori_loop(0, modes, backward, 0)
    padded[...] = jnp.zeros_like(padded)
    for p in range(6):
        padded[:n, :n] = sums[p]
        acc[p] = pltpu.roll(pltpu.roll(padded[...], r, 0), c, 1)


def position_terms(corner, extended, probe_modes, measured_one, tables):
    layers, n = extended.shape[0], probe_modes.shape[-1]
    modes = probe_modes.shape[1]
    wide = extended.shape[-1]
    vmem = pl.BlockSpec(memory_space=pltpu.VMEM)
    return pl.pallas_call(
        position_kernel,
        out_shape=jax.ShapeDtypeStruct((6, wide, wide), jnp.float32),
        in_specs=[pl.BlockSpec(memory_space=pltpu.SMEM)] + [vmem] * 4,
        out_specs=vmem,
        scratch_shapes=[
            pltpu.VMEM((4, n, n), jnp.float32),
            pltpu.VMEM((2, modes, n, n), jnp.float32),
            pltpu.VMEM((2, modes, n, n), jnp.float32),
            pltpu.VMEM((n, n), jnp.float32),
            pltpu.VMEM((6, n, n), jnp.float32),
            pltpu.VMEM((wide, wide), jnp.float32),
        ],
        compiler_params=pltpu.CompilerParams(vmem_limit_bytes=60 * 1024 * 1024),
        name="position_terms",
    )(corner, extended, probe_modes, measured_one, tables)


def from_behind(array, axis, by):
    count = lax.axis_size(axis)
    pairs = [(i, i + by) for i in range(count) if 0 <= i + by < count]
    return lax.ppermute(array, axis, pairs)


def extend_tile(current, rim_width):
    below_rim = from_behind(current[:, :, :rim_width, :], "tx", -1)
    taller = jnp.concatenate([current, below_rim], axis=2)
    right_rim = from_behind(taller[:, :, :, :rim_width], "ty", -1)
    return jnp.concatenate([taller, right_rim], axis=3)


def return_rims(accumulated, tile_side, rim_width):
    spilled = from_behind(accumulated[:, :, :, tile_side:], "ty", 1)
    narrowed = accumulated[:, :, :, :tile_side].at[:, :, :, :rim_width].add(spilled)
    lower_rim = from_behind(narrowed[:, :, tile_side:, :], "tx", 1)
    return narrowed[:, :, :tile_side, :].at[:, :, :rim_width, :].add(lower_rim)


def on_device(object_slices, probe_modes, corners, measured):
    layers = object_slices.shape[0]
    tile_side = object_slices.shape[2]
    pixels = probe_modes.shape[-1]
    rim_width = pixels // 2
    positions = corners.shape[2]
    share_rows = tile_side // lax.axis_size("scan")
    wide = tile_side + rim_width
    tables = jnp.asarray(dft_tables(pixels))
    current = object_slices
    extended = extend_tile(current, rim_width).reshape(2 * layers, wide, wide)
    accumulated = sum(
        position_terms(
            corners[0, 0, position], extended, probe_modes, measured[0, 0, position], tables
        )
        for position in range(positions)
    ).reshape(layers, 3, wide, wide)
    shared = lax.psum_scatter(
        return_rims(accumulated, tile_side, rim_width), "scan", scatter_dimension=2, tiled=True
    )
    row_first = lax.axis_index("scan") * share_rows
    own_rows = lax.dynamic_slice_in_dim(current, row_first, share_rows, 2)
    own_new = own_rows - step_size * shared[:, :2] / (shared[:, 2:3] + 1.0)
    return lax.all_gather(own_new, "scan", axis=2, tiled=True)


def solution(mesh):
    placed = (
        P(None, None, "tx", "ty"),
        P(),
        P("tx", "ty", "scan", None),
        P("tx", "ty", "scan", None, None),
    )
    return jax.shard_map(
        on_device, mesh=mesh, in_specs=placed, out_specs=P(None, None, "tx", "ty"), check_vma=False
    )
```

```python
import functools
import math

import jax
import jax.numpy as jnp
import numpy as np
from jax import lax
from jax.experimental import pallas as pl
from jax.experimental.pallas import tpu as pltpu
from jax.sharding import PartitionSpec as P

fresnel_coef = 0.1
step_size = 4.0
damping = 0.5 * fresnel_coef**2


def dft_tables(pixels):
    half = pixels // 2
    tables = []
    for parity in range(2):
        freq = 2 * np.arange(half) + parity
        angle = 2.0 * np.pi * ((freq[:, None] * np.arange(half)[None, :]) % pixels) / pixels
        c, s = np.cos(angle) / math.sqrt(pixels), np.sin(angle) / math.sqrt(pixels)
        tables.append(np.block([[c, s], [-s, c]]))
    tables += [t.T for t in tables]
    out = []
    for t in tables:
        t32 = t.astype(np.float32)
        high = t32.astype(jnp.bfloat16)
        low = (t - high.astype(np.float64)).astype(np.float32).astype(jnp.bfloat16)
        out += [high, low]
    return np.stack(out)


def split2(x):
    high = x.astype(jnp.bfloat16)
    return high, (x - high.astype(jnp.float32)).astype(jnp.bfloat16)


def right_dot(x, high, low):
    xh, xl = split2(x)
    lhs = jnp.concatenate([xh, xl, xh], axis=1)
    rhs = jnp.concatenate([high, high, low], axis=0)
    return jnp.dot(lhs, rhs, preferred_element_type=jnp.float32)


def left_dot(high, low, x):
    xh, xl = split2(x)
    lhs = jnp.concatenate([high, high, low], axis=1)
    rhs = jnp.concatenate([xh, xl, xh], axis=0)
    return jnp.dot(lhs, rhs, preferred_element_type=jnp.float32)


def propagate(re, im, sign, edges):
    first_row, last_row, first_col, last_col = edges
    n = re.shape[0]

    def lap(v):
        up = jnp.where(first_row, 0.0, pltpu.roll(v, 1, 0))
        down = jnp.where(last_row, 0.0, pltpu.roll(v, n - 1, 0))
        left = jnp.where(first_col, 0.0, pltpu.roll(v, 1, 1))
        right = jnp.where(last_col, 0.0, pltpu.roll(v, n - 1, 1))
        return (up + down) + (left + right) - 4.0 * v

    l_re, l_im = lap(re), lap(im)
    ll_re, ll_im = lap(l_re), lap(l_im)
    coef = sign * fresnel_coef
    return re - coef * l_im - damping * ll_re, im + coef * l_re - damping * ll_im


def position_kernel(
    corner, ext, probe, measured, tables, acc, trans, wave1, far, misfit, sums, padded
):
    modes, n = probe.shape[1], probe.shape[2]
    h = n // 2
    r, c = corner[0], corner[1]
    wide = ext.shape[2]
    up, left = jnp.where(r == 0, 0, wide - r), jnp.where(c == 0, 0, wide - c)
    for p in range(4):
        rows = pltpu.roll(ext[p], up, 0)[:n]
        window = pltpu.roll(rows, left, 1)[:, :n]
        trans[p] = window + 1.0 if p % 2 == 0 else window
    row = lax.broadcasted_iota(jnp.int32, (n, n), 0)
    col = lax.broadcasted_iota(jnp.int32, (n, n), 1)
    edges = (row == 0, row == n - 1, col == 0, col == n - 1)
    one_hot = jnp.where(col == jnp.where(row < h, 2 * row, 2 * (row - h) + 1), 1.0, 0.0)
    one_hot_t = jnp.where(row == jnp.where(col < h, 2 * col, 2 * (col - h) + 1), 1.0, 0.0)

    def three(x):
        hi, rest = split2(x)
        mid = rest
        lo = (x - hi.astype(jnp.float32) - mid.astype(jnp.float32)).astype(jnp.bfloat16)
        return hi, mid, lo

    ph, pt = one_hot.astype(jnp.bfloat16), one_hot_t.astype(jnp.bfloat16)
    half_done = sum(
        jnp.dot(ph, part, preferred_element_type=jnp.float32) for part in three(measured[...])
    )
    misfit[...] = -sum(
        jnp.dot(part, pt, preferred_element_type=jnp.float32) for part in three(half_done)
    )
    sums[...] = jnp.zeros_like(sums)

    def forward(m, _):
        re0, im0 = probe[0, m], probe[1, m]
        sums[2] += re0 * re0 + im0 * im0
        tr, ti = trans[0], trans[1]
        re1, im1 = propagate(re0 * tr - im0 * ti, re0 * ti + im0 * tr, 1.0, edges)
        wave1[0, m] = re1
        wave1[1, m] = im1
        sums[5] += re1 * re1 + im1 * im1
        tr, ti = trans[2], trans[3]
        er, ei = re1 * tr - im1 * ti, re1 * ti + im1 * tr
        even = right_dot(
            jnp.concatenate([er[:, :h] + er[:, h:], ei[:, :h] + ei[:, h:]], axis=1),
            tables[4], tables[5],
        )
        odd = right_dot(
            jnp.concatenate([er[:, :h] - er[:, h:], ei[:, :h] - ei[:, h:]], axis=1),
            tables[6], tables[7],
        )
        fr = jnp.concatenate([even[:, :h], odd[:, :h]], axis=1)
        fi = jnp.concatenate([even[:, h:], odd[:, h:]], axis=1)
        f_even = left_dot(
            tables[0], tables[1],
            jnp.concatenate([fr[:h] + fr[h:], fi[:h] + fi[h:]], axis=0),
        )
        f_odd = left_dot(
            tables[2], tables[3],
            jnp.concatenate([fr[:h] - fr[h:], fi[:h] - fi[h:]], axis=0),
        )
        far[0, m] = f_even
        far[1, m] = f_odd
        misfit[:h] += f_even[:h] * f_even[:h] + f_even[h:] * f_even[h:]
        misfit[h:] += f_odd[:h] * f_odd[:h] + f_odd[h:] * f_odd[h:]
        return 0

    lax.fori_loop(0, modes, forward, 0)

    def backward(m, _):
        m_even, m_odd = 2.0 * misfit[:h], 2.0 * misfit[h:]
        b_even = left_dot(
            tables[4], tables[5], far[0, m] * jnp.concatenate([m_even, m_even], axis=0)
        )
        b_odd = left_dot(
            tables[6], tables[7], far[1, m] * jnp.concatenate([m_odd, m_odd], axis=0)
        )
        top, low = b_even + b_odd, b_even - b_odd
        br = jnp.concatenate([top[:h], low[:h]], axis=0)
        bi = jnp.concatenate([top[h:], low[h:]], axis=0)
        c_even = right_dot(
            jnp.concatenate([br[:, :h], bi[:, :h]], axis=1), tables[0], tables[1]
        )
        c_odd = right_dot(
            jnp.concatenate([br[:, h:], bi[:, h:]], axis=1), tables[2], tables[3]
        )
        lo, hi = c_even + c_odd, c_even - c_odd
        br = jnp.concatenate([lo[:, :h], hi[:, :h]], axis=1)
        bi = jnp.concatenate([lo[:, h:], hi[:, h:]], axis=1)
        wr, wi = wave1[0, m], wave1[1, m]
        sums[3] += wr * br + wi * bi
        sums[4] += wr * bi - wi * br
        tr, ti = trans[2], trans[3]
        br, bi = propagate(tr * br + ti * bi, tr * bi - ti * br, -1.0, edges)
        wr, wi = probe[0, m], probe[1, m]
        sums[0] += wr * br + wi * bi
        sums[1] += wr * bi - wi * br
        return 0

    lax.fori_loop(0, modes, backward, 0)
    padded[...] = jnp.zeros_like(padded)
    for p in range(6):
        padded[:n, :n] = sums[p]
        acc[p] = pltpu.roll(pltpu.roll(padded[...], r, 0), c, 1)


def position_terms(corner, extended, probe_modes, measured_one, tables):
    layers, n = extended.shape[0], probe_modes.shape[-1]
    modes = probe_modes.shape[1]
    wide = extended.shape[-1]
    vmem = pl.BlockSpec(memory_space=pltpu.VMEM)
    return pl.pallas_call(
        position_kernel,
        out_shape=jax.ShapeDtypeStruct((6, wide, wide), jnp.float32),
        in_specs=[pl.BlockSpec(memory_space=pltpu.SMEM)] + [vmem] * 4,
        out_specs=vmem,
        scratch_shapes=[
            pltpu.VMEM((4, n, n), jnp.float32),
            pltpu.VMEM((2, modes, n, n), jnp.float32),
            pltpu.VMEM((2, modes, n, n), jnp.float32),
            pltpu.VMEM((n, n), jnp.float32),
            pltpu.VMEM((6, n, n), jnp.float32),
            pltpu.VMEM((wide, wide), jnp.float32),
        ],
        compiler_params=pltpu.CompilerParams(vmem_limit_bytes=60 * 1024 * 1024),
        name="position_terms",
    )(corner, extended, probe_modes, measured_one, tables)


MESH = pl.DeviceIdType.MESH


def meet(neighbours):
    barrier = pltpu.get_barrier_semaphore()
    for there, target in neighbours:

        @pl.when(there)
        def _():
            pl.semaphore_signal(barrier, inc=1, device_id=target, device_id_type=MESH)

    pl.semaphore_wait(barrier, sum(there.astype(jnp.int32) for there, _ in neighbours))


def fetch_kernel(n_tx, n_ty, tile, ext, send_sem, recv_sem):
    tx, ty = lax.axis_index("tx"), lax.axis_index("ty")
    side, wide = tile.shape[1], ext.shape[1]
    rim = wide - side
    up, left = tx > 0, ty > 0
    down, right = tx + 1 < n_tx, ty + 1 < n_ty
    tx_up, ty_left = jnp.maximum(tx - 1, 0), jnp.maximum(ty - 1, 0)
    tx_down, ty_right = jnp.minimum(tx + 1, n_tx - 1), jnp.minimum(ty + 1, n_ty - 1)
    meet([
        (up, {"tx": tx_up}),
        (down, {"tx": tx_down}),
        (left, {"ty": ty_left}),
        (right, {"ty": ty_right}),
        (up & left, {"tx": tx_up, "ty": ty_left}),
        (down & right, {"tx": tx_down, "ty": ty_right}),
    ])

    def rim_copy(slot, source, place, target):
        return pltpu.make_async_remote_copy(
            src_ref=source, dst_ref=place, send_sem=send_sem.at[slot], recv_sem=recv_sem.at[slot],
            device_id=target, device_id_type=MESH,
        )

    near, far = pl.ds(0, side), pl.ds(side, rim)
    first = pl.ds(0, rim)
    copies = [
        (up, down, rim_copy(0, tile.at[:, first, :], ext.at[:, far, near], {"tx": tx_up}), far, near),
        (
            up & left, down & right,
            rim_copy(1, tile.at[:, first, first], ext.at[:, far, far], {"tx": tx_up, "ty": ty_left}),
            far, far,
        ),
        (left, right, rim_copy(2, tile.at[:, :, first], ext.at[:, near, far], {"ty": ty_left}), near, far),
    ]
    for sends, _, copy, _, _ in copies:

        @pl.when(sends)
        def _():
            copy.start()

    ext[:, near, near] = tile[...]
    for _, gets, _, rows, cols in copies:

        @pl.when(jnp.logical_not(gets))
        def _():
            ext[:, rows, cols] = jnp.zeros((tile.shape[0], rows.size, cols.size), jnp.float32)

    for sends, gets, copy, _, _ in copies:

        @pl.when(gets)
        def _():
            copy.wait_recv()

        @pl.when(sends)
        def _():
            copy.wait_send()


def extend_tile(tile, rim, n_tx, n_ty):
    wide = tile.shape[1] + rim
    vmem = pl.BlockSpec(memory_space=pltpu.VMEM)
    return pl.pallas_call(
        functools.partial(fetch_kernel, n_tx, n_ty),
        out_shape=jax.ShapeDtypeStruct((tile.shape[0], wide, wide), jnp.float32),
        in_specs=[vmem],
        out_specs=vmem,
        scratch_shapes=[pltpu.SemaphoreType.DMA((3,)), pltpu.SemaphoreType.DMA((3,))],
        compiler_params=pltpu.CompilerParams(collective_id=0, has_side_effects=True),
        name="fetch_rims",
    )(tile)


def reduce_kernel(
    n, n_tx, n_ty, acc, tile, out, ty_buf, tx_buf, work, rs_buf, fresh,
    rim_send, rim_recv, rs_send, rs_recv, ag_send, ag_recv,
):
    me, tx, ty = lax.axis_index("scan"), lax.axis_index("tx"), lax.axis_index("ty")
    side, wide = tile.shape[1], acc.shape[1]
    rim = wide - side
    up, left = tx > 0, ty > 0
    down, right = tx + 1 < n_tx, ty + 1 < n_ty
    tx_up, ty_left = jnp.maximum(tx - 1, 0), jnp.maximum(ty - 1, 0)
    tx_down, ty_right = jnp.minimum(tx + 1, n_tx - 1), jnp.minimum(ty + 1, n_ty - 1)
    peers = [lax.rem(me + d, n) for d in range(1, n)]
    meet(
        [
            (up, {"tx": tx_up}),
            (down, {"tx": tx_down}),
            (left, {"ty": ty_left}),
            (right, {"ty": ty_right}),
        ]
        + [(me >= 0, {"scan": peer}) for peer in peers]
    )

    def rim_copy(slot, source, place, target):
        return pltpu.make_async_remote_copy(
            src_ref=source, dst_ref=place, send_sem=rim_send.at[slot], recv_sem=rim_recv.at[slot],
            device_id=target, device_id_type=MESH,
        )

    to_right = [
        rim_copy(slot, acc.at[:, rows, pl.ds(side, rim)], ty_buf.at[:, rows, :], {"ty": ty_right})
        for slot, rows in enumerate((pl.ds(side, rim), pl.ds(0, side)))
    ]
    to_below = rim_copy(2, work.at[:, pl.ds(side, rim), :], tx_buf, {"tx": tx_down})

    @pl.when(right)
    def _():
        to_right[0].start()
        to_right[1].start()

    work[:, side:, :] = acc[:, side:, :side]

    @pl.when(left)
    def _():
        to_right[0].wait_recv()
        work[:, side:, :rim] += ty_buf[:, side:, :]

    @pl.when(down)
    def _():
        to_below.start()

    work[:, :side, :] = acc[:, :side, :side]

    @pl.when(left)
    def _():
        to_right[1].wait_recv()
        work[:, :side, :rim] += ty_buf[:, :side, :]

    starts = (rim, 0)
    counts = ((side - rim) // n, rim // n)

    def rows_of(part, owner):
        return pl.ds(pl.multiple_of(starts[part] + owner * counts[part], 8), counts[part])

    def share_copy(part, d):
        return pltpu.make_async_remote_copy(
            src_ref=work.at[:, rows_of(part, peers[d]), :],
            dst_ref=rs_buf.at[d, :, pl.ds(part * counts[0], counts[part]), :],
            send_sem=rs_send.at[part, d], recv_sem=rs_recv.at[part, d],
            device_id={"scan": peers[d]}, device_id_type=MESH,
        )

    def fresh_copy(part, d):
        return pltpu.make_async_remote_copy(
            src_ref=fresh.at[:, pl.ds(part * counts[0], counts[part]), :],
            dst_ref=out.at[:, rows_of(part, me), :],
            send_sem=ag_send.at[part, d], recv_sem=ag_recv.at[part, d],
            device_id={"scan": peers[d]}, device_id_type=MESH,
        )

    def finish(part):
        own = rows_of(part, me)
        kept = pl.ds(part * counts[0], counts[part])
        total = work[:, own, :]
        for d in range(n - 1):
            share_copy(part, d).wait_recv()
            total = total + rs_buf[d, :, kept, :]
        for p in range(tile.shape[0]):
            base = p // 2 * 3
            new = tile[p, own, :] - step_size * total[base + p % 2] / (total[base + 2] + 1.0)
            fresh[p, kept, :] = new
            out[p, own, :] = new
        for d in range(n - 1):
            fresh_copy(part, d).start()

    for d in range(n - 1):
        share_copy(0, d).start()

    @pl.when(up)
    def _():
        to_below.wait_recv()
        work[:, :rim, :] += tx_buf[...]

    for d in range(n - 1):
        share_copy(1, d).start()
    finish(0)
    finish(1)
    for part in range(2):
        for d in range(n - 1):
            fresh_copy(part, d).wait_recv()
    for part in range(2):
        for d in range(n - 1):
            share_copy(part, d).wait_send()
            fresh_copy(part, d).wait_send()

    @pl.when(right)
    def _():
        to_right[0].wait_send()
        to_right[1].wait_send()

    @pl.when(down)
    def _():
        to_below.wait_send()


def reduce_and_update(acc, tile, n, n_tx, n_ty):
    planes, wide, _ = acc.shape
    side = tile.shape[1]
    rim = wide - side
    own = side // n
    vmem = pl.BlockSpec(memory_space=pltpu.VMEM)
    dma = pltpu.SemaphoreType.DMA
    return pl.pallas_call(
        functools.partial(reduce_kernel, n, n_tx, n_ty),
        out_shape=jax.ShapeDtypeStruct(tile.shape, jnp.float32),
        in_specs=[vmem, vmem],
        out_specs=vmem,
        scratch_shapes=[
            pltpu.VMEM((planes, wide, rim), jnp.float32),
            pltpu.VMEM((planes, rim, side), jnp.float32),
            pltpu.VMEM((planes, wide, side), jnp.float32),
            pltpu.VMEM((n - 1, planes, own, side), jnp.float32),
            pltpu.VMEM((tile.shape[0], own, side), jnp.float32),
            dma((3,)), dma((3,)),
            dma((2, n - 1)), dma((2, n - 1)), dma((2, n - 1)), dma((2, n - 1)),
        ],
        compiler_params=pltpu.CompilerParams(collective_id=1, has_side_effects=True),
        name="reduce_update",
    )(acc, tile)


def on_device(n_scan, n_tx, n_ty, object_slices, probe_modes, corners, measured):
    layers = object_slices.shape[0]
    tile_side = object_slices.shape[2]
    pixels = probe_modes.shape[-1]
    positions = corners.shape[2]
    tables = jnp.asarray(dft_tables(pixels))
    tile = object_slices.reshape(2 * layers, tile_side, tile_side)
    extended = extend_tile(tile, pixels // 2, n_tx, n_ty)
    accumulated = sum(
        position_terms(
            corners[0, 0, position], extended, probe_modes, measured[0, 0, position], tables
        )
        for position in range(positions)
    )
    updated = reduce_and_update(accumulated, tile, n_scan, n_tx, n_ty)
    return updated.reshape(object_slices.shape)


def solution(mesh):
    placed = (
        P(None, None, "tx", "ty"),
        P(),
        P("tx", "ty", "scan", None),
        P("tx", "ty", "scan", None, None),
    )
    sizes = (mesh.shape["scan"], mesh.shape["tx"], mesh.shape["ty"])
    return jax.shard_map(
        functools.partial(on_device, *sizes),
        mesh=mesh,
        in_specs=placed,
        out_specs=P(None, None, "tx", "ty"),
        check_vma=False,
    )
```

```python
import functools
import math

import jax
import jax.numpy as jnp
import numpy as np
from jax import lax
from jax.experimental import pallas as pl
from jax.experimental.pallas import tpu as pltpu
from jax.sharding import PartitionSpec as P

fresnel_coef = 0.1
step_size = 4.0
damping = 0.5 * fresnel_coef**2


def dft_tables(pixels):
    half = pixels // 2
    tables = []
    for parity in range(2):
        freq = 2 * np.arange(half) + parity
        angle = 2.0 * np.pi * ((freq[:, None] * np.arange(half)[None, :]) % pixels) / pixels
        c, s = np.cos(angle) / math.sqrt(pixels), np.sin(angle) / math.sqrt(pixels)
        tables.append(np.block([[c, s], [-s, c]]))
    tables += [t.T for t in tables]
    out = []
    for t in tables:
        t32 = t.astype(np.float32)
        high = t32.astype(jnp.bfloat16)
        low = (t - high.astype(np.float64)).astype(np.float32).astype(jnp.bfloat16)
        out += [high, low]
    return np.stack(out)


def split2(x):
    high = x.astype(jnp.bfloat16)
    return high, (x - high.astype(jnp.float32)).astype(jnp.bfloat16)


def right_dot(x, high, low):
    xh, xl = split2(x)
    lhs = jnp.concatenate([xh, xl, xh], axis=1)
    rhs = jnp.concatenate([high, high, low], axis=0)
    return jnp.dot(lhs, rhs, preferred_element_type=jnp.float32)


def left_dot(high, low, x):
    xh, xl = split2(x)
    lhs = jnp.concatenate([high, high, low], axis=1)
    rhs = jnp.concatenate([xh, xl, xh], axis=0)
    return jnp.dot(lhs, rhs, preferred_element_type=jnp.float32)


def propagate(re, im, sign, edges):
    first_row, last_row, first_col, last_col = edges
    n = re.shape[0]

    def lap(v):
        up = jnp.where(first_row, 0.0, pltpu.roll(v, 1, 0))
        down = jnp.where(last_row, 0.0, pltpu.roll(v, n - 1, 0))
        left = jnp.where(first_col, 0.0, pltpu.roll(v, 1, 1))
        right = jnp.where(last_col, 0.0, pltpu.roll(v, n - 1, 1))
        return (up + down) + (left + right) - 4.0 * v

    l_re, l_im = lap(re), lap(im)
    ll_re, ll_im = lap(l_re), lap(l_im)
    coef = sign * fresnel_coef
    return re - coef * l_im - damping * ll_re, im + coef * l_re - damping * ll_im


def position_kernel(
    corner, ext, probe, measured, tables, acc, trans, wave1, far, misfit, sums, padded
):
    modes, n = probe.shape[1], probe.shape[2]
    h = n // 2
    r, c = corner[0], corner[1]
    wide = ext.shape[2]
    up, left = jnp.where(r == 0, 0, wide - r), jnp.where(c == 0, 0, wide - c)
    for p in range(4):
        rows = pltpu.roll(ext[p], up, 0)[:n]
        window = pltpu.roll(rows, left, 1)[:, :n]
        trans[p] = window + 1.0 if p % 2 == 0 else window
    row = lax.broadcasted_iota(jnp.int32, (n, n), 0)
    col = lax.broadcasted_iota(jnp.int32, (n, n), 1)
    edges = (row == 0, row == n - 1, col == 0, col == n - 1)
    one_hot = jnp.where(col == jnp.where(row < h, 2 * row, 2 * (row - h) + 1), 1.0, 0.0)
    one_hot_t = jnp.where(row == jnp.where(col < h, 2 * col, 2 * (col - h) + 1), 1.0, 0.0)

    def three(x):
        hi, rest = split2(x)
        mid = rest
        lo = (x - hi.astype(jnp.float32) - mid.astype(jnp.float32)).astype(jnp.bfloat16)
        return hi, mid, lo

    ph, pt = one_hot.astype(jnp.bfloat16), one_hot_t.astype(jnp.bfloat16)
    half_done = sum(
        jnp.dot(ph, part, preferred_element_type=jnp.float32) for part in three(measured[...])
    )
    misfit[...] = -sum(
        jnp.dot(part, pt, preferred_element_type=jnp.float32) for part in three(half_done)
    )
    sums[...] = jnp.zeros_like(sums)

    def forward(m, _):
        re0, im0 = probe[0, m], probe[1, m]
        sums[2] += re0 * re0 + im0 * im0
        tr, ti = trans[0], trans[1]
        re1, im1 = propagate(re0 * tr - im0 * ti, re0 * ti + im0 * tr, 1.0, edges)
        wave1[0, m] = re1
        wave1[1, m] = im1
        sums[5] += re1 * re1 + im1 * im1
        tr, ti = trans[2], trans[3]
        er, ei = re1 * tr - im1 * ti, re1 * ti + im1 * tr
        even = right_dot(
            jnp.concatenate([er[:, :h] + er[:, h:], ei[:, :h] + ei[:, h:]], axis=1),
            tables[4], tables[5],
        )
        odd = right_dot(
            jnp.concatenate([er[:, :h] - er[:, h:], ei[:, :h] - ei[:, h:]], axis=1),
            tables[6], tables[7],
        )
        fr = jnp.concatenate([even[:, :h], odd[:, :h]], axis=1)
        fi = jnp.concatenate([even[:, h:], odd[:, h:]], axis=1)
        f_even = left_dot(
            tables[0], tables[1],
            jnp.concatenate([fr[:h] + fr[h:], fi[:h] + fi[h:]], axis=0),
        )
        f_odd = left_dot(
            tables[2], tables[3],
            jnp.concatenate([fr[:h] - fr[h:], fi[:h] - fi[h:]], axis=0),
        )
        far[0, m] = f_even
        far[1, m] = f_odd
        misfit[:h] += f_even[:h] * f_even[:h] + f_even[h:] * f_even[h:]
        misfit[h:] += f_odd[:h] * f_odd[:h] + f_odd[h:] * f_odd[h:]
        return 0

    lax.fori_loop(0, modes, forward, 0, unroll=2)

    def backward(m, _):
        m_even, m_odd = 2.0 * misfit[:h], 2.0 * misfit[h:]
        b_even = left_dot(
            tables[4], tables[5], far[0, m] * jnp.concatenate([m_even, m_even], axis=0)
        )
        b_odd = left_dot(
            tables[6], tables[7], far[1, m] * jnp.concatenate([m_odd, m_odd], axis=0)
        )
        top, low = b_even + b_odd, b_even - b_odd
        br = jnp.concatenate([top[:h], low[:h]], axis=0)
        bi = jnp.concatenate([top[h:], low[h:]], axis=0)
        c_even = right_dot(
            jnp.concatenate([br[:, :h], bi[:, :h]], axis=1), tables[0], tables[1]
        )
        c_odd = right_dot(
            jnp.concatenate([br[:, h:], bi[:, h:]], axis=1), tables[2], tables[3]
        )
        lo, hi = c_even + c_odd, c_even - c_odd
        br = jnp.concatenate([lo[:, :h], hi[:, :h]], axis=1)
        bi = jnp.concatenate([lo[:, h:], hi[:, h:]], axis=1)
        wr, wi = wave1[0, m], wave1[1, m]
        sums[3] += wr * br + wi * bi
        sums[4] += wr * bi - wi * br
        tr, ti = trans[2], trans[3]
        br, bi = propagate(tr * br + ti * bi, tr * bi - ti * br, -1.0, edges)
        wr, wi = probe[0, m], probe[1, m]
        sums[0] += wr * br + wi * bi
        sums[1] += wr * bi - wi * br
        return 0

    lax.fori_loop(0, modes, backward, 0, unroll=2)
    padded[...] = jnp.zeros_like(padded)
    for p in range(6):
        padded[:n, :n] = sums[p]
        acc[p] = pltpu.roll(pltpu.roll(padded[...], r, 0), c, 1)


def position_terms(corner, extended, probe_modes, measured_one, tables):
    layers, n = extended.shape[0], probe_modes.shape[-1]
    modes = probe_modes.shape[1]
    wide = extended.shape[-1]
    vmem = pl.BlockSpec(memory_space=pltpu.VMEM)
    return pl.pallas_call(
        position_kernel,
        out_shape=jax.ShapeDtypeStruct((6, wide, wide), jnp.float32),
        in_specs=[pl.BlockSpec(memory_space=pltpu.SMEM)] + [vmem] * 4,
        out_specs=vmem,
        scratch_shapes=[
            pltpu.VMEM((4, n, n), jnp.float32),
            pltpu.VMEM((2, modes, n, n), jnp.float32),
            pltpu.VMEM((2, modes, n, n), jnp.float32),
            pltpu.VMEM((n, n), jnp.float32),
            pltpu.VMEM((6, n, n), jnp.float32),
            pltpu.VMEM((wide, wide), jnp.float32),
        ],
        compiler_params=pltpu.CompilerParams(vmem_limit_bytes=60 * 1024 * 1024),
        name="position_terms",
    )(corner, extended, probe_modes, measured_one, tables)


MESH = pl.DeviceIdType.MESH


def meet(neighbours):
    barrier = pltpu.get_barrier_semaphore()
    for there, target in neighbours:

        @pl.when(there)
        def _():
            pl.semaphore_signal(barrier, inc=1, device_id=target, device_id_type=MESH)

    pl.semaphore_wait(barrier, sum(there.astype(jnp.int32) for there, _ in neighbours))


def fetch_kernel(n_tx, n_ty, tile, ext, send_sem, recv_sem):
    tx, ty = lax.axis_index("tx"), lax.axis_index("ty")
    side, wide = tile.shape[1], ext.shape[1]
    rim = wide - side
    up, left = tx > 0, ty > 0
    down, right = tx + 1 < n_tx, ty + 1 < n_ty
    tx_up, ty_left = jnp.maximum(tx - 1, 0), jnp.maximum(ty - 1, 0)
    tx_down, ty_right = jnp.minimum(tx + 1, n_tx - 1), jnp.minimum(ty + 1, n_ty - 1)
    meet([
        (up, {"tx": tx_up}),
        (down, {"tx": tx_down}),
        (left, {"ty": ty_left}),
        (right, {"ty": ty_right}),
        (up & left, {"tx": tx_up, "ty": ty_left}),
        (down & right, {"tx": tx_down, "ty": ty_right}),
    ])

    def rim_copy(slot, source, place, target):
        return pltpu.make_async_remote_copy(
            src_ref=source, dst_ref=place, send_sem=send_sem.at[slot], recv_sem=recv_sem.at[slot],
            device_id=target, device_id_type=MESH,
        )

    near, far = pl.ds(0, side), pl.ds(side, rim)
    first = pl.ds(0, rim)
    copies = [
        (up, down, rim_copy(0, tile.at[:, first, :], ext.at[:, far, near], {"tx": tx_up}), far, near),
        (
            up & left, down & right,
            rim_copy(1, tile.at[:, first, first], ext.at[:, far, far], {"tx": tx_up, "ty": ty_left}),
            far, far,
        ),
        (left, right, rim_copy(2, tile.at[:, :, first], ext.at[:, near, far], {"ty": ty_left}), near, far),
    ]
    for sends, _, copy, _, _ in copies:

        @pl.when(sends)
        def _():
            copy.start()

    ext[:, near, near] = tile[...]
    for _, gets, _, rows, cols in copies:

        @pl.when(jnp.logical_not(gets))
        def _():
            ext[:, rows, cols] = jnp.zeros((tile.shape[0], rows.size, cols.size), jnp.float32)

    for sends, gets, copy, _, _ in copies:

        @pl.when(gets)
        def _():
            copy.wait_recv()

        @pl.when(sends)
        def _():
            copy.wait_send()


def extend_tile(tile, rim, n_tx, n_ty):
    wide = tile.shape[1] + rim
    vmem = pl.BlockSpec(memory_space=pltpu.VMEM)
    return pl.pallas_call(
        functools.partial(fetch_kernel, n_tx, n_ty),
        out_shape=jax.ShapeDtypeStruct((tile.shape[0], wide, wide), jnp.float32),
        in_specs=[vmem],
        out_specs=vmem,
        scratch_shapes=[pltpu.SemaphoreType.DMA((3,)), pltpu.SemaphoreType.DMA((3,))],
        compiler_params=pltpu.CompilerParams(collective_id=0, has_side_effects=True),
        name="fetch_rims",
    )(tile)


def reduce_kernel(
    n, n_tx, n_ty, acc, tile, out, ty_buf, tx_buf, work, rs_buf, fresh,
    rim_send, rim_recv, rs_send, rs_recv, ag_send, ag_recv,
):
    me, tx, ty = lax.axis_index("scan"), lax.axis_index("tx"), lax.axis_index("ty")
    side, wide = tile.shape[1], acc.shape[1]
    rim = wide - side
    up, left = tx > 0, ty > 0
    down, right = tx + 1 < n_tx, ty + 1 < n_ty
    tx_up, ty_left = jnp.maximum(tx - 1, 0), jnp.maximum(ty - 1, 0)
    tx_down, ty_right = jnp.minimum(tx + 1, n_tx - 1), jnp.minimum(ty + 1, n_ty - 1)
    peers = [lax.rem(me + d, n) for d in range(1, n)]
    meet(
        [
            (up, {"tx": tx_up}),
            (down, {"tx": tx_down}),
            (left, {"ty": ty_left}),
            (right, {"ty": ty_right}),
        ]
        + [(me >= 0, {"scan": peer}) for peer in peers]
    )

    def rim_copy(slot, source, place, target):
        return pltpu.make_async_remote_copy(
            src_ref=source, dst_ref=place, send_sem=rim_send.at[slot], recv_sem=rim_recv.at[slot],
            device_id=target, device_id_type=MESH,
        )

    to_right = [
        rim_copy(slot, acc.at[:, rows, pl.ds(side, rim)], ty_buf.at[:, rows, :], {"ty": ty_right})
        for slot, rows in enumerate((pl.ds(side, rim), pl.ds(0, side)))
    ]
    to_below = rim_copy(2, work.at[:, pl.ds(side, rim), :], tx_buf, {"tx": tx_down})

    @pl.when(right)
    def _():
        to_right[0].start()
        to_right[1].start()

    work[:, side:, :] = acc[:, side:, :side]

    @pl.when(left)
    def _():
        to_right[0].wait_recv()
        work[:, side:, :rim] += ty_buf[:, side:, :]

    @pl.when(down)
    def _():
        to_below.start()

    work[:, :side, :] = acc[:, :side, :side]

    @pl.when(left)
    def _():
        to_right[1].wait_recv()
        work[:, :side, :rim] += ty_buf[:, :side, :]

    starts = (rim, 0)
    counts = ((side - rim) // n, rim // n)

    def rows_of(part, owner):
        return pl.ds(pl.multiple_of(starts[part] + owner * counts[part], 8), counts[part])

    def share_copy(part, d):
        return pltpu.make_async_remote_copy(
            src_ref=work.at[:, rows_of(part, peers[d]), :],
            dst_ref=rs_buf.at[d, :, pl.ds(part * counts[0], counts[part]), :],
            send_sem=rs_send.at[part, d], recv_sem=rs_recv.at[part, d],
            device_id={"scan": peers[d]}, device_id_type=MESH,
        )

    def fresh_copy(part, d):
        return pltpu.make_async_remote_copy(
            src_ref=fresh.at[:, pl.ds(part * counts[0], counts[part]), :],
            dst_ref=out.at[:, rows_of(part, me), :],
            send_sem=ag_send.at[part, d], recv_sem=ag_recv.at[part, d],
            device_id={"scan": peers[d]}, device_id_type=MESH,
        )

    def finish(part):
        own = rows_of(part, me)
        kept = pl.ds(part * counts[0], counts[part])
        total = work[:, own, :]
        for d in range(n - 1):
            share_copy(part, d).wait_recv()
            total = total + rs_buf[d, :, kept, :]
        for p in range(tile.shape[0]):
            base = p // 2 * 3
            new = tile[p, own, :] - step_size * total[base + p % 2] / (total[base + 2] + 1.0)
            fresh[p, kept, :] = new
            out[p, own, :] = new
        for d in range(n - 1):
            fresh_copy(part, d).start()

    for d in range(n - 1):
        share_copy(0, d).start()

    @pl.when(up)
    def _():
        to_below.wait_recv()
        work[:, :rim, :] += tx_buf[...]

    for d in range(n - 1):
        share_copy(1, d).start()
    finish(0)
    finish(1)
    for part in range(2):
        for d in range(n - 1):
            fresh_copy(part, d).wait_recv()
    for part in range(2):
        for d in range(n - 1):
            share_copy(part, d).wait_send()
            fresh_copy(part, d).wait_send()

    @pl.when(right)
    def _():
        to_right[0].wait_send()
        to_right[1].wait_send()

    @pl.when(down)
    def _():
        to_below.wait_send()


def reduce_and_update(acc, tile, n, n_tx, n_ty):
    planes, wide, _ = acc.shape
    side = tile.shape[1]
    rim = wide - side
    own = side // n
    vmem = pl.BlockSpec(memory_space=pltpu.VMEM)
    dma = pltpu.SemaphoreType.DMA
    return pl.pallas_call(
        functools.partial(reduce_kernel, n, n_tx, n_ty),
        out_shape=jax.ShapeDtypeStruct(tile.shape, jnp.float32),
        in_specs=[vmem, vmem],
        out_specs=vmem,
        scratch_shapes=[
            pltpu.VMEM((planes, wide, rim), jnp.float32),
            pltpu.VMEM((planes, rim, side), jnp.float32),
            pltpu.VMEM((planes, wide, side), jnp.float32),
            pltpu.VMEM((n - 1, planes, own, side), jnp.float32),
            pltpu.VMEM((tile.shape[0], own, side), jnp.float32),
            dma((3,)), dma((3,)),
            dma((2, n - 1)), dma((2, n - 1)), dma((2, n - 1)), dma((2, n - 1)),
        ],
        compiler_params=pltpu.CompilerParams(collective_id=1, has_side_effects=True),
        name="reduce_update",
    )(acc, tile)


def on_device(n_scan, n_tx, n_ty, object_slices, probe_modes, corners, measured):
    layers = object_slices.shape[0]
    tile_side = object_slices.shape[2]
    pixels = probe_modes.shape[-1]
    positions = corners.shape[2]
    tables = jnp.asarray(dft_tables(pixels))
    tile = object_slices.reshape(2 * layers, tile_side, tile_side)
    extended = extend_tile(tile, pixels // 2, n_tx, n_ty)
    accumulated = sum(
        position_terms(
            corners[0, 0, position], extended, probe_modes, measured[0, 0, position], tables
        )
        for position in range(positions)
    )
    updated = reduce_and_update(accumulated, tile, n_scan, n_tx, n_ty)
    return updated.reshape(object_slices.shape)


def solution(mesh):
    placed = (
        P(None, None, "tx", "ty"),
        P(),
        P("tx", "ty", "scan", None),
        P("tx", "ty", "scan", None, None),
    )
    sizes = (mesh.shape["scan"], mesh.shape["tx"], mesh.shape["ty"])
    return jax.shard_map(
        functools.partial(on_device, *sizes),
        mesh=mesh,
        in_specs=placed,
        out_specs=P(None, None, "tx", "ty"),
        check_vma=False,
    )
```
